256 devices in a mesh: row: 8 (over z_hi, y), col: 32 (over z_lo, x, core).
Axes of the slice: x: 4, y: 4, z: 8 (z_hi: 2, z_lo: 4; z = z_hi * 4 + z_lo), core: 2. Of those that a mesh axis runs over, the one named last changes fastest.
Arguments:
- queries: bfloat16 [32768, 256], P(('row', 'col')), may hold values from -6 to 6
- keys: bfloat16 [32768, 256], P('col', 'row'), may hold values from -6 to 6
- values: bfloat16 [32768, 256], P('col', 'row'), may hold values from -0.59765625 to 0.59765625
- outputs: bfloat16 [32768, 256], P(('row', 'col')), may hold values from -0.59765625 to 0.59765625
- d_out: bfloat16 [32768, 256], P(('row', 'col')), may hold values from -6 to 6
- lse: float32 [2, 32768], P(None, ('row', 'col')), may hold values from 4 to 6
Outputs:
- d_queries: bfloat16 [32768, 256], P(('row', 'col'))
- d_keys: bfloat16 [32768, 256], P('col', 'row')
- d_values: bfloat16 [32768, 256], P('col', 'row')
The draws below stay inside these ranges and needn't reach their ends.
All inputs are finite; a program needn't handle non-finite values.
Results may differ from the reference program's by a relative error of at most 0.0049.
Values may be sent and summed in bfloat16 or wider, within the bound.
No kernel may reach another device: no remote copies, remote signals or barrier semaphores. Data moves between devices by JAX's collectives and lax.ppermute only.
A program may use at most 64 MiB of HBM per device.

```python
import math
import jax
import jax.numpy as jnp
from jax import lax

HEAD_DIM = 128
HEADS = 2
SEQ = 32768
HD = 256


def steps_of(own_key, dims, pieces, low, largest):
    loudness, own = 1.0, jax.random.fold_in(own_key, 6)
    for dim, parts in pieces:
        draws = jnp.exp(jax.random.uniform(jax.random.fold_in(own, dim), (parts,), jnp.float32, low / len(pieces), largest / len(pieces)))
        loudness = loudness * jnp.repeat(draws, dims[dim] // parts).reshape([-1 if axis == dim else 1 for axis in range(len(dims))])
    return loudness


def scatter_about(key, dims, width, limit, shards=(), dtype=jnp.bfloat16):
    drawn = width * jax.random.normal(key, dims, jnp.float32)
    if shards:
        drawn = drawn * steps_of(key, dims, shards, -0.22, 0.18)
    return jnp.clip(drawn, -limit, limit).astype(dtype)


def setup_inputs(seed: int = 0) -> dict:
    key_of = jax.random.split(jax.random.key(seed), 7)
    return {
        "queries": scatter_about(key_of[0], (SEQ, HD), 1.0, 6.0, ((0, 256),)),
        "keys": scatter_about(key_of[1], (SEQ, HD), 1.0, 6.0, ((0, 32), (1, 8))),
        "values": scatter_about(key_of[2], (SEQ, HD), 0.1, 0.59765625, ((0, 32), (1, 8))),
        "outputs": scatter_about(key_of[3], (SEQ, HD), 0.1, 0.59765625, ((0, 256),)),
        "d_out": scatter_about(key_of[4], (SEQ, HD), 1.0, 6.0, ((0, 256),)),
        "lse": jnp.clip(4.0 + 2.0 * jax.random.uniform(key_of[5], (HEADS, SEQ), jnp.float32) ** steps_of(key_of[5], (HEADS, SEQ), ((1, 256),), -0.2, 0.2), 4.0, 6.0),
    }


def contract_rows(left, right):
    return lax.dot_general(left, right, (((0,), (0,)), ((), ())), preferred_element_type=jnp.float32)


def head_pass(query_head, key_head, value_head, grad_head, lse_head, delta_head):
    scaling = HEAD_DIM ** -0.5
    block_rows = math.gcd(SEQ, 1024)
    steps_total = SEQ // block_rows
    query_blocks = query_head.reshape(steps_total, block_rows, HEAD_DIM)
    grad_blocks = grad_head.reshape(steps_total, block_rows, HEAD_DIM)
    lse_blocks = lse_head.reshape(steps_total, block_rows)
    delta_blocks = delta_head.reshape(steps_total, block_rows)

    def advance(running, inputs):
        key_sum, value_sum = running
        query_rows, grad_rows, lse_rows, delta_rows = inputs
        scores = jnp.dot(query_rows, key_head.T, preferred_element_type=jnp.float32)
        probs = jnp.exp(scores * scaling - lse_rows[:, None])
        probs_low = probs.astype(jnp.bfloat16)
        grad_probs = jnp.dot(grad_rows, value_head.T, preferred_element_type=jnp.float32)
        grad_scores = (probs * (grad_probs - delta_rows[:, None])).astype(jnp.bfloat16)
        value_sum = value_sum + contract_rows(probs_low, grad_rows)
        key_sum = key_sum + contract_rows(grad_scores, query_rows)
        query_part = jnp.dot(grad_scores, key_head, preferred_element_type=jnp.float32)
        return (key_sum, value_sum), query_part

    empty_sums = jnp.zeros((SEQ, HEAD_DIM), jnp.float32)
    (key_sum, value_sum), query_parts = lax.scan(advance, (empty_sums, empty_sums), (query_blocks, grad_blocks, lse_blocks, delta_blocks))
    query_grad = query_parts.reshape(SEQ, HEAD_DIM) * scaling
    return query_grad, key_sum * scaling, value_sum


def reference(queries, keys, values, outputs, d_out, lse):
    product = d_out.astype(jnp.float32) * outputs.astype(jnp.float32)
    delta = jnp.sum(product.reshape(SEQ, HEADS, HEAD_DIM), axis=2).T
    query_list = []
    key_list = []
    value_list = []
    for head_index in range(HEADS):
        first_col = head_index * HEAD_DIM
        last_col = first_col + HEAD_DIM
        query_grad, key_grad, value_grad = head_pass(queries[:, first_col:last_col], keys[:, first_col:last_col], values[:, first_col:last_col], d_out[:, first_col:last_col], lse[head_index], delta[head_index])
        query_list.append(query_grad)
        key_list.append(key_grad)
        value_list.append(value_grad)
    d_queries = jnp.concatenate(query_list, axis=1).astype(jnp.bfloat16)
    d_keys = jnp.concatenate(key_list, axis=1).astype(jnp.bfloat16)
    d_values = jnp.concatenate(value_list, axis=1).astype(jnp.bfloat16)
    return (d_queries, d_keys, d_values)
```

```python
import functools
import math

import jax
import jax.numpy as jnp
from jax import lax
from jax.experimental import pallas as pl
from jax.experimental.pallas import tpu as pltpu
from jax.sharding import Mesh
from jax.sharding import PartitionSpec as P

F32 = jnp.float32
BF16 = jnp.bfloat16
HEAD_DIM = 128
ROWS = 128
KEYS = 1024
FEATS = 32
SIDE = 16
MSG = 2 * ROWS + SIDE
SCALING = HEAD_DIM ** (-0.5)
LOG2E = math.log2(math.e)
NT = (((1,), (1,)), ((), ()))
NN = (((1,), (0,)), ((), ()))
TN = (((0,), (0,)), ((), ()))
VMEM = pl.BlockSpec(memory_space=pltpu.VMEM)


def dot(left, right, dims):
    return lax.dot_general(left, right, dims, preferred_element_type=F32)


def split3(value):
    high = value.astype(BF16).astype(F32)
    middle = (value - high).astype(BF16).astype(F32)
    return high, middle, value - high - middle


def call(body, out_shape, operands, name, flops=0, moved=4 * 2**20, scratch=(), aliases=None):
    return pl.pallas_call(
        body,
        out_shape=out_shape,
        in_specs=[VMEM] * len(operands),
        out_specs=jax.tree.map(lambda _: VMEM, out_shape),
        scratch_shapes=list(scratch),
        input_output_aliases=aliases or {},
        compiler_params=pltpu.CompilerParams(vmem_limit_bytes=48 * 2**20),
        cost_estimate=pl.CostEstimate(flops=flops, bytes_accessed=moved, transcendentals=0),
        name=name,
    )(*operands)


def pack_queries(q_ref, do_ref, o_ref, lse_ref, msg_ref):
    product = do_ref[...].astype(F32) * o_ref[...].astype(F32)
    row = lax.broadcasted_iota(jnp.int32, (SIDE, ROWS), 0)
    for head in range(2):
        cols = pl.ds(head * HEAD_DIM, HEAD_DIM)
        part = product[:, head * HEAD_DIM : (head + 1) * HEAD_DIM]
        delta = jnp.sum(part.T, axis=0, keepdims=True)
        terms = split3(lse_ref[head : head + 1, :] * LOG2E) + split3(delta)
        side = jnp.zeros((SIDE, ROWS), F32)
        for index, term in enumerate(terms):
            side = jnp.where(row == index, jnp.broadcast_to(term, (SIDE, ROWS)), side)
        side = side.astype(BF16)
        for place in range(4):
            target = head * 4 + place
            msg_ref[target, 0:ROWS, :] = q_ref[:, cols]
            msg_ref[target, ROWS : 2 * ROWS, :] = do_ref[:, cols]
            msg_ref[target, 2 * ROWS : MSG, :] = side


def pack_keys(k_ref, v_ref, kv_ref):
    kv_ref[0:FEATS, :] = k_ref[...]
    kv_ref[FEATS : 2 * FEATS, :] = v_ref[...]


def join_keys(y_ref, own_ref, next_ref, prev_ref, far_ref, kv_ref, kt, vt):
    y = y_ref[0]
    for shift, ref in ((0, own_ref), (3, prev_ref), (1, next_ref), (2, far_ref)):
        source = lax.rem(y + shift, 4)
        rows = pl.ds(pl.multiple_of(source * FEATS, FEATS), FEATS)
        kt[rows, :] = ref[0:FEATS, :].astype(F32)
        vt[rows, :] = ref[FEATS : 2 * FEATS, :].astype(F32)
    kv_ref[0] = kt[...].T.astype(BF16)
    kv_ref[1] = vt[...].T.astype(BF16)


def attend(halves, tile, with_dq, last, fresh, *refs):
    refs = list(refs)
    msg_ref = refs.pop(0)
    kv_refs = [refs.pop(0) for _ in range(halves)]
    acc_in = [None if fresh else refs.pop(0) for _ in range(halves)]
    dq_in = refs.pop(0) if with_dq else None
    dq_out = refs.pop(0)
    acc_out = [refs.pop(0) for _ in range(halves)]
    q_s, do_s, st_s, dq_s = refs
    for place in range(8):
        rows = pl.ds(place * ROWS, ROWS)
        q_s[rows, :] = msg_ref[place, 0:ROWS, :]
        do_s[rows, :] = msg_ref[place, ROWS : 2 * ROWS, :]
        side = msg_ref[place, 2 * ROWS : MSG, :].astype(F32)
        st_s[0:1, rows] = side[0:1] + side[1:2] + side[2:3]
        st_s[1:2, rows] = side[3:4] + side[4:5] + side[5:6]
    if with_dq:
        dq_s[...] = dq_in[...]
    else:
        dq_s[...] = jnp.zeros_like(dq_s)
    total = 8 * ROWS
    for half in range(halves):
        kv_ref, accum_in, accum_out = kv_refs[half], acc_in[half], acc_out[half]

        def step(index, _, kv_ref=kv_ref, accum_in=accum_in, accum_out=accum_out):
            ks = pl.ds(pl.multiple_of(index * tile, tile), tile)
            key, value = kv_ref[0, ks, :], kv_ref[1, ks, :]
            if accum_in is None:
                dk = dv = jnp.zeros((tile, HEAD_DIM), F32)
            else:
                dk, dv = accum_in[0, ks, :], accum_in[1, ks, :]
            for start in range(0, total, 256):
                qs = pl.ds(start, 256)
                query, grad = q_s[qs, :], do_s[qs, :]
                scores = dot(key, query, NT)
                probs = jnp.exp2(scores * (SCALING * LOG2E) - st_s[0:1, qs])
                grad_probs = dot(value, grad, NT)
                grad_scores = (probs * (grad_probs - st_s[1:2, qs])).astype(BF16)
                dv = dv + dot(probs.astype(BF16), grad, NN)
                dk = dk + dot(grad_scores, query, NN)
                dq_s[qs, :] += dot(grad_scores, key, TN)
            accum_out[0, ks, :] = dk
            accum_out[1, ks, :] = dv
            return 0

        lax.fori_loop(0, KEYS // tile, step, 0)
    if last:
        for place in range(8):
            dq_out[place] = dq_s[pl.ds(place * ROWS, ROWS), :].astype(BF16)
    else:
        dq_out[...] = dq_s[...]


def attend_call(msg, kvs, accs, dq_in, last, name):
    halves = len(kvs)
    fresh = accs is None
    operands = [msg] + list(kvs) + ([] if fresh else list(accs))
    aliases = {} if fresh else {1 + halves + i: 1 + i for i in range(halves)}
    if dq_in is not None:
        operands.append(dq_in)
    if last:
        dq_shape = jax.ShapeDtypeStruct((8, ROWS, HEAD_DIM), BF16)
    else:
        dq_shape = jax.ShapeDtypeStruct((8 * ROWS, HEAD_DIM), F32)
    out = (dq_shape,) + (jax.ShapeDtypeStruct((2, KEYS, HEAD_DIM), F32),) * halves
    body = functools.partial(attend, halves, 1024, dq_in is not None, last, fresh)
    results = call(
        body,
        out,
        operands,
        name,
        flops=halves * 10 * 1024 * 1024 * 128,
        moved=halves * 8 * 2**20,
        scratch=[
            pltpu.VMEM((8 * ROWS, HEAD_DIM), BF16),
            pltpu.VMEM((8 * ROWS, HEAD_DIM), BF16),
            pltpu.VMEM((8, 8 * ROWS), F32),
            pltpu.VMEM((8 * ROWS, HEAD_DIM), F32),
        ],
        aliases=aliases,
    )
    return results[0], results[1:]


def add_queries(own_ref, a_ref, b_ref, c_ref, out_ref):
    total = own_ref[...].astype(F32) + a_ref[...].astype(F32)
    total = total + b_ref[...].astype(F32) + c_ref[...].astype(F32)
    out_ref[...] = total.astype(BF16)


def finish_queries(in_ref, out_ref):
    for head in range(2):
        total = in_ref[head * 4].astype(F32)
        for place in range(1, 4):
            total = total + in_ref[head * 4 + place].astype(F32)
        out_ref[:, head * HEAD_DIM : (head + 1) * HEAD_DIM] = (total * SCALING).astype(BF16)


def pack_sums(core_ref, own_ref, other_ref, out_ref):
    core = core_ref[0]
    for index, ref in ((core, own_ref), (1 - core, other_ref)):
        dk = (ref[0] * SCALING).T.astype(BF16)
        dv = ref[1].T.astype(BF16)
        for y in range(4):
            rows = slice(y * FEATS, (y + 1) * FEATS)
            out_ref[2 * y + index, 0:FEATS, :] = dk[rows]
            out_ref[2 * y + index, FEATS : 2 * FEATS, :] = dv[rows]


def finish_keys(in_ref, dk_ref, dv_ref):
    total = in_ref[0].astype(F32)
    for place in range(1, 8):
        total = total + in_ref[place].astype(F32)
    dk_ref[...] = total[0:FEATS].astype(BF16)
    dv_ref[...] = total[FEATS : 2 * FEATS].astype(BF16)


def shift(value, axis, size, amount):
    return lax.ppermute(value, axis, [(i, (i + amount) % size) for i in range(size)])


def per_device(queries, keys, values, outputs, d_out, lse):
    sds = jax.ShapeDtypeStruct
    y = lax.axis_index("y").astype(jnp.int32).reshape(1)
    core = lax.axis_index("c").astype(jnp.int32).reshape(1)
    smem = pl.BlockSpec(memory_space=pltpu.SMEM)

    kvt = call(pack_keys, sds((2 * FEATS, KEYS), BF16), [keys.T, values.T], "pack_keys")
    kv_next = shift(kvt, "y", 4, 3)
    kv_prev = shift(kvt, "y", 4, 1)
    kv_far = shift(kvt, "y", 4, 2)

    msg = call(
        pack_queries, sds((8, MSG, HEAD_DIM), BF16), [queries, d_out, outputs, lse], "pack_queries"
    )
    q_own = lax.all_to_all(msg, ("zh", "zl"), 0, 0, tiled=True)
    q_prev = shift(q_own, "x", 4, 1)
    q_next = shift(q_own, "x", 4, 3)
    cut = MSG // 2
    q_far = jnp.concatenate(
        [shift(q_prev[:, :cut], "x", 4, 1), shift(q_next[:, cut:], "x", 4, 3)], axis=1
    )

    kv_own = pl.pallas_call(
        join_keys,
        out_shape=sds((2, KEYS, HEAD_DIM), BF16),
        in_specs=[smem] + [VMEM] * 4,
        out_specs=VMEM,
        scratch_shapes=[pltpu.VMEM((HEAD_DIM, KEYS), F32)] * 2,
        name="join_keys",
    )(y, kvt, kv_next, kv_prev, kv_far)
    kv_other = shift(kv_own, "c", 2, 1)

    dq0, (acc_own,) = attend_call(q_own, [kv_own], None, None, False, "attend_own_a")
    dq0, (acc_other,) = attend_call(q_own, [kv_other], None, dq0, True, "attend_own_b")
    kvs = [kv_own, kv_other]
    dq_p, accs = attend_call(q_prev, kvs, [acc_own, acc_other], None, True, "attend_prev")
    dq_n, accs = attend_call(q_next, kvs, accs, None, True, "attend_next")
    dq_f, accs = attend_call(q_far, kvs, accs, None, True, "attend_far")
    back_p = shift(dq_p, "x", 4, 3)
    back_n = shift(dq_n, "x", 4, 1)
    back_f = shift(dq_f, "x", 4, 2)

    sums = pl.pallas_call(
        pack_sums,
        out_shape=sds((8, 2 * FEATS, KEYS), BF16),
        in_specs=[smem] + [VMEM] * 2,
        out_specs=VMEM,
        name="pack_sums",
    )(core, *accs)
    sums = lax.all_to_all(sums, ("y", "c"), 0, 0, tiled=True)
    dq = call(
        add_queries, sds((8, ROWS, HEAD_DIM), BF16), [dq0, back_p, back_n, back_f], "add_queries"
    )
    dq = lax.all_to_all(dq, ("zh", "zl"), 0, 0, tiled=True)
    d_queries = call(finish_queries, sds((ROWS, 2 * HEAD_DIM), BF16), [dq], "finish_queries")
    d_keys, d_values = call(
        finish_keys, (sds((FEATS, KEYS), BF16),) * 2, [sums], "finish_keys"
    )
    return d_queries, d_keys.T, d_values.T


def solution(mesh):
    every = ("zh", "y", "zl", "x", "c")
    fine = Mesh(mesh.devices.reshape(2, 4, 4, 4, 2), every)
    placed = (
        P(every, None),
        P(("zl", "x", "c"), ("zh", "y")),
        P(("zl", "x", "c"), ("zh", "y")),
        P(every, None),
        P(every, None),
        P(None, every),
    )
    return jax.shard_map(
        per_device,
        mesh=fine,
        in_specs=placed,
        out_specs=(placed[0], placed[1], placed[2]),
        check_vma=False,
    )
```

```python
import functools
import math

import jax
import jax.numpy as jnp
from jax import lax
from jax.experimental import pallas as pl
from jax.experimental.pallas import tpu as pltpu
from jax.sharding import Mesh
from jax.sharding import PartitionSpec as P

F32 = jnp.float32
BF16 = jnp.bfloat16
HEAD_DIM = 128
ROWS = 128
KEYS = 1024
FEATS = 32
SIDE = 16
MSG = 2 * ROWS + SIDE
SCALING = HEAD_DIM ** (-0.5)
LOG2E = math.log2(math.e)
NT = (((1,), (1,)), ((), ()))
NN = (((1,), (0,)), ((), ()))
TN = (((0,), (0,)), ((), ()))
VMEM = pl.BlockSpec(memory_space=pltpu.VMEM)
SMEM = pl.BlockSpec(memory_space=pltpu.SMEM)


def dot(left, right, dims):
    return lax.dot_general(left, right, dims, preferred_element_type=F32)


def split3(value):
    high = value.astype(BF16).astype(F32)
    middle = (value - high).astype(BF16).astype(F32)
    return high, middle, value - high - middle


def call(body, out_shape, operands, name, flops=0, moved=1024, scratch=(), aliases=None, scalars=0, limit=8):
    return pl.pallas_call(
        body,
        out_shape=out_shape,
        in_specs=[SMEM] * scalars + [VMEM] * (len(operands) - scalars),
        out_specs=jax.tree.map(lambda _: VMEM, out_shape),
        scratch_shapes=list(scratch),
        input_output_aliases=aliases or {},
        compiler_params=pltpu.CompilerParams(vmem_limit_bytes=limit * 2**20),
        cost_estimate=pl.CostEstimate(flops=flops, bytes_accessed=moved, transcendentals=0),
        name=name,
    )(*operands)


def prepare(q_hbm, do_hbm, o_hbm, lse_hbm, k_hbm, v_hbm, msg_ref, kv_ref, q_s, do_s, o_s, lse_s, sems):
    copies = [
        pltpu.make_async_copy(do_hbm, do_s, sems.at[0]),
        pltpu.make_async_copy(o_hbm, o_s, sems.at[1]),
        pltpu.make_async_copy(lse_hbm, lse_s, sems.at[2]),
        pltpu.make_async_copy(q_hbm, q_s, sems.at[3]),
        pltpu.make_async_copy(k_hbm, kv_ref.at[pl.ds(0, FEATS)], sems.at[4]),
        pltpu.make_async_copy(v_hbm, kv_ref.at[pl.ds(FEATS, FEATS)], sems.at[5]),
    ]
    for copy in copies:
        copy.start()
    for copy in copies[:4]:
        copy.wait()
    product = do_s[...].astype(F32) * o_s[...].astype(F32)
    row = lax.broadcasted_iota(jnp.int32, (SIDE, ROWS), 0)
    for head in range(2):
        cols = pl.ds(head * HEAD_DIM, HEAD_DIM)
        part = product[:, head * HEAD_DIM : (head + 1) * HEAD_DIM]
        delta = jnp.sum(part.T, axis=0, keepdims=True)
        terms = split3(lse_s[head : head + 1, :] * LOG2E) + split3(delta)
        side = jnp.zeros((SIDE, ROWS), F32)
        for index, term in enumerate(terms):
            side = jnp.where(row == index, jnp.broadcast_to(term, (SIDE, ROWS)), side)
        side = side.astype(BF16)
        for place in range(4):
            target = head * 4 + place
            msg_ref[target, 0:ROWS, :] = q_s[:, cols]
            msg_ref[target, ROWS : 2 * ROWS, :] = do_s[:, cols]
            msg_ref[target, 2 * ROWS : MSG, :] = side
    for copy in copies[4:]:
        copy.wait()


def join_keys(y_ref, own_ref, next_ref, prev_ref, far_ref, k_ref, v_ref, kt, vt):
    y = y_ref[0]
    for shift, ref in ((0, own_ref), (3, prev_ref), (1, next_ref), (2, far_ref)):
        source = lax.rem(y + shift, 4)
        rows = pl.ds(pl.multiple_of(source * FEATS, FEATS), FEATS)
        kt[rows, :] = ref[0:FEATS, :]
        vt[rows, :] = ref[FEATS : 2 * FEATS, :]
    k_ref[...] = kt[...].T
    v_ref[...] = vt[...].T


def attend(first, last, blocks, *refs):
    refs = list(refs)
    core_ref = refs.pop(0) if last else None
    msg_refs = [refs.pop(0), refs.pop(0)]
    k_ref, v_ref = refs.pop(0), refs.pop(0)
    dq_in = None if first else refs.pop(0)
    dq_out = refs.pop(0)
    sums_ref, q_s, do_s, st_s, dk_s, dv_s = refs[:6]
    dq_s = refs[6] if last else dq_out
    for index in range(16):
        msg_ref, place = msg_refs[index // 8], index % 8
        span = pl.ds(index * ROWS, ROWS)
        q_s[span, :] = msg_ref[place, 0:ROWS, :]
        do_s[span, :] = msg_ref[place, ROWS : 2 * ROWS, :]
        side = msg_ref[place, 2 * ROWS : MSG, :].astype(F32)
        st_s[0:1, span] = side[0:1] + side[1:2] + side[2:3]
        st_s[1:2, span] = side[3:4] + side[4:5] + side[5:6]
    dk_s[...] = jnp.zeros_like(dk_s)
    dv_s[...] = jnp.zeros_like(dv_s)
    key, value = k_ref[...], v_ref[...]

    def step(index, _):
        for block in range(blocks):
            qs = pl.ds(pl.multiple_of(index * blocks * 256 + block * 256, 256), 256)
            query, grad = q_s[qs, :], do_s[qs, :]
            scores = dot(key, query, NT)
            probs = jnp.exp2(scores * (SCALING * LOG2E) - st_s[0:1, qs])
            grad_probs = dot(value, grad, NT)
            grad_scores = (probs * (grad_probs - st_s[1:2, qs])).astype(BF16)
            dv_s[...] += dot(probs.astype(BF16), grad, NN)
            dk_s[...] += dot(grad_scores, query, NN)
            dq = dot(grad_scores, key, TN)
            dq_s[qs, :] = dq if first else dq_in[qs, :] + dq
        return 0

    if blocks == 8:
        step(0, 0)
    else:
        lax.fori_loop(0, 8 // blocks, step, 0)
    if last:
        core = core_ref[0]
        for index in range(16):
            slot = 2 * (index % 8) + (core if index < 8 else 1 - core)
            dq_out[slot] = dq_s[pl.ds(index * ROWS, ROWS), :].astype(BF16)
    dk = (dk_s[...] * SCALING).astype(BF16).T
    dv = dv_s[...].astype(BF16).T
    for y in range(4):
        rows = slice(y * FEATS, (y + 1) * FEATS)
        sums_ref[2 * y * FEATS : (2 * y + 1) * FEATS, :] = dk[rows]
        sums_ref[(2 * y + 1) * FEATS : (2 * y + 2) * FEATS, :] = dv[rows]


def attend_call(msgs, chunk, dq_in, name, core=None, weight=0, blocks=4):
    sds = jax.ShapeDtypeStruct
    first = dq_in is None
    last = core is not None
    operands = ([core] if last else []) + list(msgs) + list(chunk) + ([] if first else [dq_in])
    if last:
        out = (sds((16, ROWS, HEAD_DIM), BF16),)
    else:
        out = (sds((16 * ROWS, HEAD_DIM), F32),)
    out += (sds((8 * FEATS, KEYS), BF16),)
    return call(
        functools.partial(attend, first, last, blocks),
        out,
        operands,
        name,
        flops=int(weight * 10 * 2**27),
        moved=int(weight * 2**23),
        scratch=[
            pltpu.VMEM((16 * ROWS, HEAD_DIM), BF16),
            pltpu.VMEM((16 * ROWS, HEAD_DIM), BF16),
            pltpu.VMEM((8, 16 * ROWS), F32),
            pltpu.VMEM((KEYS, HEAD_DIM), F32),
            pltpu.VMEM((KEYS, HEAD_DIM), F32),
        ]
        + [pltpu.VMEM((16 * ROWS, HEAD_DIM), F32)] * last,
        scalars=int(last),
        limit=30,
    )


def finish_queries(in_ref, out_ref):
    for head in range(2):
        total = in_ref[head * 8].astype(F32)
        for place in range(1, 8):
            total = total + in_ref[head * 8 + place].astype(F32)
        out_ref[:, head * HEAD_DIM : (head + 1) * HEAD_DIM] = (total * SCALING).astype(BF16)


def pack_sums(y_ref, own_ref, a_ref, b_ref, c_ref, mine_ref, next_ref, prev_ref, far_ref, total):
    y = y_ref[0]
    partial = own_ref[...].astype(F32) + a_ref[...].astype(F32)
    total[...] = partial + b_ref[...].astype(F32) + c_ref[...].astype(F32)
    for shift, ref in ((0, mine_ref), (1, next_ref), (3, prev_ref), (2, far_ref)):
        target = lax.rem(y + shift, 4)
        ref[...] = total[pl.ds(pl.multiple_of(target * 2 * FEATS, 2 * FEATS), 2 * FEATS), :].astype(BF16)


def finish_keys(a_ref, b_ref, c_ref, d_ref, dk_ref, dv_ref):
    total = a_ref[...].astype(F32) + b_ref[...].astype(F32)
    total = total + c_ref[...].astype(F32) + d_ref[...].astype(F32)
    dk_ref[...] = total[0:FEATS].astype(BF16)
    dv_ref[...] = total[FEATS : 2 * FEATS].astype(BF16)


def shift(value, axis, size, amount):
    return lax.ppermute(value, axis, [(i, (i + amount) % size) for i in range(size)])


X = ("xa", "xb")
Z = ("zh", "zl")


def per_device(queries, keys, values, outputs, d_out, lse):
    sds = jax.ShapeDtypeStruct
    y = lax.axis_index("y").astype(jnp.int32).reshape(1)
    core = lax.axis_index("c").astype(jnp.int32).reshape(1)

    msg, kvt = pl.pallas_call(
        prepare,
        out_shape=(sds((8, MSG, HEAD_DIM), BF16), sds((2 * FEATS, KEYS), BF16)),
        in_specs=[pl.BlockSpec(memory_space=pl.ANY)] * 6,
        out_specs=(VMEM, VMEM),
        scratch_shapes=[pltpu.VMEM((ROWS, 2 * HEAD_DIM), BF16)] * 3
        + [pltpu.VMEM((2, ROWS), F32), pltpu.SemaphoreType.DMA((6,))],
        cost_estimate=pl.CostEstimate(flops=0, bytes_accessed=2**20, transcendentals=0),
        name="prepare",
    )(queries, d_out, outputs, lse, keys.T, values.T)
    q_own = lax.all_to_all(msg, Z, 0, 0, tiled=True)
    kv_next = shift(kvt, "y", 4, 3)
    kv_prev = shift(kvt, "y", 4, 1)
    kv_far = shift(kvt, "y", 4, 2)
    k_own, v_own = call(
        join_keys,
        (sds((KEYS, HEAD_DIM), BF16),) * 2,
        [y, kvt, kv_next, kv_prev, kv_far],
        "join_keys",
        flops=20 * 2**30,
        scratch=[pltpu.VMEM((HEAD_DIM, KEYS), BF16)] * 2,
        scalars=1,
    )
    k_prev = shift(k_own, X, 4, 1)
    v_next = shift(v_own, X, 4, 3)
    v_prev = shift(v_own, X, 4, 1)
    k_next = shift(k_own, X, 4, 3)
    k_far = shift(k_prev, X, 4, 1)
    v_far = shift(v_next, X, 4, 3)
    q_own, k_prev, v_next, v_prev, k_next = lax.optimization_barrier(
        (q_own, k_prev, v_next, v_prev, k_next)
    )
    q_other = shift(q_own, "c", 2, 1)

    msgs = [q_own, q_other]
    dq, sums_prev = attend_call(msgs, [k_prev, v_prev], None, "attend_prev")
    back_prev = shift(sums_prev, X, 4, 3)
    dq, sums_far = attend_call(msgs, [k_far, v_far], dq, "attend_far")
    back_far = shift(sums_far, X, 4, 2)
    dq, sums_next = attend_call(msgs, [k_next, v_next], dq, "attend_next")
    back_next = shift(sums_next, X, 4, 1)
    dq, sums_own = attend_call(msgs, [k_own, v_own], dq, "attend_own", core=core, blocks=8)
    dq, back_far = lax.optimization_barrier((dq, back_far))
    dq = lax.all_to_all(dq, Z + ("c",), 0, 0, tiled=True)

    mine, to_next, to_prev, to_far = call(
        pack_sums,
        (sds((2 * FEATS, KEYS), BF16),) * 4,
        [y, sums_own, back_prev, back_far, back_next],
        "pack_sums",
        flops=100 * 2**30,
        scratch=[pltpu.VMEM((8 * FEATS, KEYS), F32)],
        scalars=1,
    )
    sums = [mine, shift(to_next, "y", 4, 1), shift(to_prev, "y", 4, 3), shift(to_far, "y", 4, 2)]
    d_queries = call(finish_queries, sds((ROWS, 2 * HEAD_DIM), BF16), [dq], "finish_queries")
    d_keys, d_values = call(
        finish_keys, (sds((FEATS, KEYS), BF16),) * 2, sums, "finish_keys"
    )
    return d_queries, d_keys.T, d_values.T


def solution(mesh):
    every = ("zh", "y", "zl", "xa", "xb", "c")
    fine = Mesh(mesh.devices.reshape(2, 4, 4, 2, 2, 2), every)
    blocks = P(("zl", "xa", "xb", "c"), ("zh", "y"))
    rows = P(every, None)
    return jax.shard_map(
        per_device,
        mesh=fine,
        in_specs=(rows, blocks, blocks, rows, rows, P(None, every)),
        out_specs=(rows, blocks, blocks),
        check_vma=False,
    )
```

```python
import functools
import math

import jax
import jax.numpy as jnp
from jax import lax
from jax.experimental import pallas as pl
from jax.experimental.pallas import tpu as pltpu
from jax.sharding import Mesh
from jax.sharding import PartitionSpec as P

F32 = jnp.float32
BF16 = jnp.bfloat16
HEAD_DIM = 128
ROWS = 128
KEYS = 1024
FEATS = 32
SIDE = 8
MSG = 2 * ROWS + SIDE
SCALING = HEAD_DIM ** (-0.5)
LOG2E = math.log2(math.e)
NT = (((1,), (1,)), ((), ()))
NN = (((1,), (0,)), ((), ()))
TN = (((0,), (0,)), ((), ()))
VMEM = pl.BlockSpec(memory_space=pltpu.VMEM)
SMEM = pl.BlockSpec(memory_space=pltpu.SMEM)


def dot(left, right, dims):
    return lax.dot_general(left, right, dims, preferred_element_type=F32)


def split3(value):
    high = value.astype(BF16).astype(F32)
    middle = (value - high).astype(BF16).astype(F32)
    return high, middle, value - high - middle


def call(body, out_shape, operands, name, flops=0, moved=1024, scratch=(), aliases=None, scalars=0, limit=8):
    return pl.pallas_call(
        body,
        out_shape=out_shape,
        in_specs=[SMEM] * scalars + [VMEM] * (len(operands) - scalars),
        out_specs=jax.tree.map(lambda _: VMEM, out_shape),
        scratch_shapes=list(scratch),
        input_output_aliases=aliases or {},
        compiler_params=pltpu.CompilerParams(vmem_limit_bytes=limit * 2**20),
        cost_estimate=pl.CostEstimate(flops=flops, bytes_accessed=moved, transcendentals=0),
        name=name,
    )(*operands)


def prepare(q_hbm, do_hbm, o_hbm, lse_hbm, k_hbm, v_hbm, msg_ref, kv_ref, q_s, do_s, o_s, lse_s, sems):
    copies = [
        pltpu.make_async_copy(do_hbm, do_s, sems.at[0]),
        pltpu.make_async_copy(o_hbm, o_s, sems.at[1]),
        pltpu.make_async_copy(lse_hbm, lse_s, sems.at[2]),
        pltpu.make_async_copy(q_hbm, q_s, sems.at[3]),
        pltpu.make_async_copy(k_hbm, kv_ref.at[pl.ds(0, FEATS)], sems.at[4]),
        pltpu.make_async_copy(v_hbm, kv_ref.at[pl.ds(FEATS, FEATS)], sems.at[5]),
    ]
    for copy in copies:
        copy.start()
    for copy in copies[:4]:
        copy.wait()
    product = do_s[...].astype(F32) * o_s[...].astype(F32)
    row = lax.broadcasted_iota(jnp.int32, (SIDE, ROWS), 0)
    for head in range(2):
        cols = pl.ds(head * HEAD_DIM, HEAD_DIM)
        part = product[:, head * HEAD_DIM : (head + 1) * HEAD_DIM]
        delta = jnp.sum(part.T, axis=0, keepdims=True)
        terms = split3(lse_s[head : head + 1, :] * LOG2E) + split3(delta)
        side = jnp.zeros((SIDE, ROWS), F32)
        for index, term in enumerate(terms):
            side = jnp.where(row == index, jnp.broadcast_to(term, (SIDE, ROWS)), side)
        side = side.astype(BF16)
        for place in range(4):
            target = head * 4 + place
            msg_ref[target, 0:ROWS, :] = q_s[:, cols]
            msg_ref[target, ROWS : 2 * ROWS, :] = do_s[:, cols]
            msg_ref[target, 2 * ROWS : MSG, :] = side
    for copy in copies[4:]:
        copy.wait()


def join_keys(y_ref, own_ref, next_ref, prev_ref, far_ref, kv_ref, kt, vt):
    y = y_ref[0]
    for shift, ref in ((0, own_ref), (3, prev_ref), (1, next_ref), (2, far_ref)):
        source = lax.rem(y + shift, 4)
        rows = pl.ds(pl.multiple_of(source * FEATS, FEATS), FEATS)
        kt[rows, :] = ref[0:FEATS, :]
        vt[rows, :] = ref[FEATS : 2 * FEATS, :]
    kv_ref[0] = kt[...].T
    kv_ref[1] = vt[...].T


def attend(first, last, blocks, *refs):
    refs = list(refs)
    core_ref = refs.pop(0) if last else None
    msg_refs = [refs.pop(0), refs.pop(0)]
    kv_ref = refs.pop(0)
    dq_in = None if first else refs.pop(0)
    dq_out = refs.pop(0)
    sums_ref, dk_s, dv_s = refs[:3]
    dq_s = refs[3] if last else dq_out
    dk_s[...] = jnp.zeros_like(dk_s)
    dv_s[...] = jnp.zeros_like(dv_s)
    key, value = kv_ref[0], kv_ref[1]

    def pair(msg_ref, place, start, size):
        return jnp.concatenate(
            [msg_ref[place, start : start + size, :], msg_ref[place + 1, start : start + size, :]],
            axis=0 if size == ROWS else 1,
        )

    def step(index, _):
        for block in range(blocks):
            which = block % 2
            place = index * blocks + block - which
            msg_ref = msg_refs[which]
            query, grad = pair(msg_ref, place, 0, ROWS), pair(msg_ref, place, ROWS, ROWS)
            side = pair(msg_ref, place, 2 * ROWS, SIDE).astype(F32)
            lse = side[0:1] + side[1:2] + side[2:3]
            delta = side[3:4] + side[4:5] + side[5:6]
            scores = dot(key, query, NT)
            probs = jnp.exp2(scores * (SCALING * LOG2E) - lse)
            grad_probs = dot(value, grad, NT)
            grad_scores = (probs * (grad_probs - delta)).astype(BF16)
            dv_s[...] += dot(probs.astype(BF16), grad, NN)
            dk_s[...] += dot(grad_scores, query, NN)
            dq = dot(grad_scores, key, TN)
            rows = pl.ds(pl.multiple_of(which * 8 * ROWS + place * ROWS, 256), 256)
            dq_s[rows, :] = dq if first else dq_in[rows, :] + dq
        return 0

    if blocks == 8:
        step(0, 0)
    else:
        lax.fori_loop(0, 8 // blocks, step, 0)
    if last:
        core = core_ref[0]
        for index in range(16):
            slot = 2 * (index % 8) + (core if index < 8 else 1 - core)
            dq_out[slot] = dq_s[pl.ds(index * ROWS, ROWS), :].astype(BF16)
    dk = (dk_s[...] * SCALING).astype(BF16).T
    dv = dv_s[...].astype(BF16).T
    for y in range(4):
        rows = slice(y * FEATS, (y + 1) * FEATS)
        sums_ref[2 * y * FEATS : (2 * y + 1) * FEATS, :] = dk[rows]
        sums_ref[(2 * y + 1) * FEATS : (2 * y + 2) * FEATS, :] = dv[rows]


def attend_call(msgs, chunk, dq_in, name, core=None, weight=0, blocks=8):
    sds = jax.ShapeDtypeStruct
    first = dq_in is None
    last = core is not None
    operands = ([core] if last else []) + list(msgs) + [chunk] + ([] if first else [dq_in])
    if last:
        out = (sds((16, ROWS, HEAD_DIM), BF16),)
    else:
        out = (sds((16 * ROWS, HEAD_DIM), F32),)
    out += (sds((8 * FEATS, KEYS), BF16),)
    return call(
        functools.partial(attend, first, last, blocks),
        out,
        operands,
        name,
        flops=int(weight * 10 * 2**27),
        moved=int(weight * 2**23),
        scratch=[
            pltpu.VMEM((KEYS, HEAD_DIM), F32),
            pltpu.VMEM((KEYS, HEAD_DIM), F32),
        ]
        + [pltpu.VMEM((16 * ROWS, HEAD_DIM), F32)] * last,
        scalars=int(last),
        limit=30,
    )


def finish_queries(in_ref, out_ref):
    for head in range(2):
        total = in_ref[head * 8].astype(F32)
        for place in range(1, 8):
            total = total + in_ref[head * 8 + place].astype(F32)
        out_ref[:, head * HEAD_DIM : (head + 1) * HEAD_DIM] = (total * SCALING).astype(BF16)


def add_sums(a_ref, b_ref, out_ref):
    out_ref[...] = a_ref[...].astype(F32) + b_ref[...].astype(F32)


def pack_sums(y_ref, near_ref, own_ref, back_ref, mine_ref, next_ref, prev_ref, far_ref, total):
    y = y_ref[0]
    total[...] = near_ref[...] + own_ref[...].astype(F32) + back_ref[...].astype(F32)
    for shift, ref in ((0, mine_ref), (1, next_ref), (3, prev_ref), (2, far_ref)):
        target = lax.rem(y + shift, 4)
        ref[...] = total[pl.ds(pl.multiple_of(target * 2 * FEATS, 2 * FEATS), 2 * FEATS), :].astype(BF16)


def finish_keys(a_ref, b_ref, c_ref, d_ref, dk_ref, dv_ref):
    total = a_ref[...].astype(F32) + b_ref[...].astype(F32)
    total = total + c_ref[...].astype(F32) + d_ref[...].astype(F32)
    dk_ref[...] = total[0:FEATS].astype(BF16)
    dv_ref[...] = total[FEATS : 2 * FEATS].astype(BF16)


def shift(value, axis, size, amount):
    return lax.ppermute(value, axis, [(i, (i + amount) % size) for i in range(size)])


X = ("xa", "xb")
Z = ("zh", "zl")


def per_device(queries, keys, values, outputs, d_out, lse):
    sds = jax.ShapeDtypeStruct
    y = lax.axis_index("y").astype(jnp.int32).reshape(1)
    core = lax.axis_index("c").astype(jnp.int32).reshape(1)

    msg, kvt = pl.pallas_call(
        prepare,
        out_shape=(sds((8, MSG, HEAD_DIM), BF16), sds((2 * FEATS, KEYS), BF16)),
        in_specs=[pl.BlockSpec(memory_space=pl.ANY)] * 6,
        out_specs=(VMEM, VMEM),
        scratch_shapes=[pltpu.VMEM((ROWS, 2 * HEAD_DIM), BF16)] * 3
        + [pltpu.VMEM((2, ROWS), F32), pltpu.SemaphoreType.DMA((6,))],
        cost_estimate=pl.CostEstimate(flops=0, bytes_accessed=2**20, transcendentals=0),
        name="prepare",
    )(queries, d_out, outputs, lse, keys.T, values.T)
    q_own = lax.all_to_all(msg, Z, 0, 0, tiled=True)
    kv_next = shift(kvt, "y", 4, 3)
    kv_prev = shift(kvt, "y", 4, 1)
    kv_far = shift(kvt, "y", 4, 2)
    kv_own = call(
        join_keys,
        sds((2, KEYS, HEAD_DIM), BF16),
        [y, kvt, kv_next, kv_prev, kv_far],
        "join_keys",
        flops=20 * 2**30,
        scratch=[pltpu.VMEM((HEAD_DIM, KEYS), BF16)] * 2,
        scalars=1,
    )
    kv_x_prev = shift(kv_own, X, 4, 1)
    kv_x_next = shift(kv_own, X, 4, 3)
    kv_x_far = shift(kv_own, X, 4, 2)
    q_own, kv_x_prev, kv_x_next = lax.optimization_barrier((q_own, kv_x_prev, kv_x_next))
    q_other = shift(q_own, "c", 2, 1)

    msgs = [q_own, q_other]
    dq, sums_prev = attend_call(msgs, kv_x_prev, None, "attend_prev")
    back_prev = shift(sums_prev, X, 4, 3)
    dq, sums_next = attend_call(msgs, kv_x_next, dq, "attend_next")
    back_next = shift(sums_next, X, 4, 1)
    dq, sums_far = attend_call(msgs, kv_x_far, dq, "attend_far")
    back_far = shift(sums_far, X, 4, 2)
    dq, sums_own = attend_call(msgs, kv_own, dq, "attend_own", core=core)
    dq, back_prev = lax.optimization_barrier((dq, back_prev))
    dq = lax.all_to_all(dq, Z + ("c",), 0, 0, tiled=True)

    near = call(
        add_sums,
        sds((8 * FEATS, KEYS), F32),
        [back_prev, back_next],
        "add_sums",
        flops=2**37,
    )
    mine, to_next, to_prev, to_far = call(
        pack_sums,
        (sds((2 * FEATS, KEYS), BF16),) * 4,
        [y, near, sums_own, back_far],
        "pack_sums",
        scratch=[pltpu.VMEM((8 * FEATS, KEYS), F32)],
        scalars=1,
    )
    sums = [mine, shift(to_next, "y", 4, 1), shift(to_prev, "y", 4, 3), shift(to_far, "y", 4, 2)]
    d_queries = call(finish_queries, sds((ROWS, 2 * HEAD_DIM), BF16), [dq], "finish_queries")
    d_keys, d_values = call(
        finish_keys, (sds((FEATS, KEYS), BF16),) * 2, sums, "finish_keys"
    )
    return d_queries, d_keys.T, d_values.T


def solution(mesh):
    every = ("zh", "y", "zl", "xa", "xb", "c")
    fine = Mesh(mesh.devices.reshape(2, 4, 4, 2, 2, 2), every)
    blocks = P(("zl", "xa", "xb", "c"), ("zh", "y"))
    rows = P(every, None)
    return jax.shard_map(
        per_device,
        mesh=fine,
        in_specs=(rows, blocks, blocks, rows, rows, P(None, every)),
        out_specs=(rows, blocks, blocks),
        check_vma=False,
    )
```

```python
import functools
import math

import jax
import jax.numpy as jnp
from jax import lax
from jax.experimental import pallas as pl
from jax.experimental.pallas import tpu as pltpu
from jax.sharding import Mesh
from jax.sharding import PartitionSpec as P

F32 = jnp.float32
BF16 = jnp.bfloat16
HEAD_DIM = 128
ROWS = 128
KEYS = 1024
FEATS = 32
SIDE = 8
MSG = 2 * ROWS + SIDE
SCALING = HEAD_DIM ** (-0.5)
LOG2E = math.log2(math.e)
NT = (((1,), (1,)), ((), ()))
NN = (((1,), (0,)), ((), ()))
TN = (((0,), (0,)), ((), ()))
VMEM = pl.BlockSpec(memory_space=pltpu.VMEM)
SMEM = pl.BlockSpec(memory_space=pltpu.SMEM)


def dot(left, right, dims):
    return lax.dot_general(left, right, dims, preferred_element_type=F32)


def split3(value):
    high = value.astype(BF16).astype(F32)
    middle = (value - high).astype(BF16).astype(F32)
    return high, middle, value - high - middle


def call(body, out_shape, operands, name, flops=0, moved=1024, scratch=(), aliases=None, scalars=0, limit=8):
    return pl.pallas_call(
        body,
        out_shape=out_shape,
        in_specs=[SMEM] * scalars + [VMEM] * (len(operands) - scalars),
        out_specs=jax.tree.map(lambda _: VMEM, out_shape),
        scratch_shapes=list(scratch),
        input_output_aliases=aliases or {},
        compiler_params=pltpu.CompilerParams(vmem_limit_bytes=limit * 2**20),
        cost_estimate=pl.CostEstimate(flops=flops, bytes_accessed=moved, transcendentals=0),
        name=name,
    )(*operands)


def prepare(q_hbm, do_hbm, o_hbm, lse_hbm, k_hbm, v_hbm, msg_ref, kv_ref, q_s, do_s, o_s, lse_s, sems):
    copies = [
        pltpu.make_async_copy(do_hbm, do_s, sems.at[0]),
        pltpu.make_async_copy(o_hbm, o_s, sems.at[1]),
        pltpu.make_async_copy(lse_hbm, lse_s, sems.at[2]),
        pltpu.make_async_copy(q_hbm, q_s, sems.at[3]),
        pltpu.make_async_copy(k_hbm, kv_ref.at[pl.ds(0, FEATS)], sems.at[4]),
        pltpu.make_async_copy(v_hbm, kv_ref.at[pl.ds(FEATS, FEATS)], sems.at[5]),
    ]
    for copy in copies:
        copy.start()
    for copy in copies[:4]:
        copy.wait()
    product = do_s[...].astype(F32) * o_s[...].astype(F32)
    row = lax.broadcasted_iota(jnp.int32, (SIDE, ROWS), 0)
    for head in range(2):
        cols = pl.ds(head * HEAD_DIM, HEAD_DIM)
        part = product[:, head * HEAD_DIM : (head + 1) * HEAD_DIM]
        delta = jnp.sum(part.T, axis=0, keepdims=True)
        terms = split3(lse_s[head : head + 1, :] * LOG2E) + split3(delta)
        side = jnp.zeros((SIDE, ROWS), F32)
        for index, term in enumerate(terms):
            side = jnp.where(row == index, jnp.broadcast_to(term, (SIDE, ROWS)), side)
        side = side.astype(BF16)
        for place in range(4):
            target = head * 4 + place
            msg_ref[target, 0:ROWS, :] = q_s[:, cols]
            msg_ref[target, ROWS : 2 * ROWS, :] = do_s[:, cols]
            msg_ref[target, 2 * ROWS : MSG, :] = side
    for copy in copies[4:]:
        copy.wait()


def join_keys(y_ref, own_ref, next_ref, prev_ref, far_ref, kv_ref, kt, vt):
    y = y_ref[0]
    for shift, ref in ((0, own_ref), (3, prev_ref), (1, next_ref), (2, far_ref)):
        source = lax.rem(y + shift, 4)
        rows = pl.ds(pl.multiple_of(source * FEATS, FEATS), FEATS)
        kt[rows, :] = ref[0:FEATS, :]
        vt[rows, :] = ref[FEATS : 2 * FEATS, :]
    kv_ref[0] = kt[...].T
    kv_ref[1] = vt[...].T


def attend(first, last, blocks, *refs):
    refs = list(refs)
    core_ref = refs.pop(0) if last else None
    msg_refs = [refs.pop(0), refs.pop(0)]
    kv_ref = refs.pop(0)
    dq_in = None if first else refs.pop(0)
    dq_out = refs.pop(0)
    sums_ref, dk_s, dv_s = refs[:3]
    dq_s = refs[3] if last else dq_out
    dk_s[...] = jnp.zeros_like(dk_s)
    dv_s[...] = jnp.zeros_like(dv_s)
    key, value = kv_ref[0], kv_ref[1]

    def pair(msg_ref, place, start, size):
        return jnp.concatenate(
            [msg_ref[place, start : start + size, :], msg_ref[place + 1, start : start + size, :]],
            axis=0 if size == ROWS else 1,
        )

    def step(index, _):
        for block in range(blocks):
            which = block % 2
            place = index * blocks + block - which
            msg_ref = msg_refs[which]
            query, grad = pair(msg_ref, place, 0, ROWS), pair(msg_ref, place, ROWS, ROWS)
            side = pair(msg_ref, place, 2 * ROWS, SIDE).astype(F32)
            lse = side[0:1] + side[1:2] + side[2:3]
            delta = side[3:4] + side[4:5] + side[5:6]
            scores = dot(key, query, NT)
            probs = jnp.exp2(scores * (SCALING * LOG2E) - lse)
            grad_probs = dot(value, grad, NT)
            grad_scores = (probs * (grad_probs - delta)).astype(BF16)
            dv_s[...] += dot(probs.astype(BF16), grad, NN)
            dk_s[...] += dot(grad_scores, query, NN)
            dq = dot(grad_scores, key, TN)
            rows = pl.ds(pl.multiple_of(which * 8 * ROWS + place * ROWS, 256), 256)
            dq_s[rows, :] = dq if first else dq_in[rows, :] + dq
        return 0

    if blocks == 8:
        step(0, 0)
    else:
        lax.fori_loop(0, 8 // blocks, step, 0)
    if last:
        core = core_ref[0]
        for index in range(16):
            slot = 2 * (index % 8) + (core if index < 8 else 1 - core)
            dq_out[slot] = dq_s[pl.ds(index * ROWS, ROWS), :].astype(BF16)
    dk = (dk_s[...] * SCALING).astype(BF16).T
    dv = dv_s[...].astype(BF16).T
    for y in range(4):
        rows = slice(y * FEATS, (y + 1) * FEATS)
        sums_ref[2 * y * FEATS : (2 * y + 1) * FEATS, :] = dk[rows]
        sums_ref[(2 * y + 1) * FEATS : (2 * y + 2) * FEATS, :] = dv[rows]


def attend_call(msgs, chunk, dq_in, name, core=None, weight=0, blocks=8):
    sds = jax.ShapeDtypeStruct
    first = dq_in is None
    last = core is not None
    operands = ([core] if last else []) + list(msgs) + [chunk] + ([] if first else [dq_in])
    if last:
        out = (sds((16, ROWS, HEAD_DIM), BF16),)
    else:
        out = (sds((16 * ROWS, HEAD_DIM), F32),)
    out += (sds((8 * FEATS, KEYS), BF16),)
    return call(
        functools.partial(attend, first, last, blocks),
        out,
        operands,
        name,
        flops=int(weight * 10 * 2**27),
        moved=int(weight * 2**23),
        scratch=[
            pltpu.VMEM((KEYS, HEAD_DIM), F32),
            pltpu.VMEM((KEYS, HEAD_DIM), F32),
        ]
        + [pltpu.VMEM((16 * ROWS, HEAD_DIM), F32)] * last,
        scalars=int(last),
        limit=30,
    )


def finish_queries(in_ref, out_ref):
    for head in range(2):
        total = in_ref[head * 8].astype(F32)
        for place in range(1, 8):
            total = total + in_ref[head * 8 + place].astype(F32)
        out_ref[:, head * HEAD_DIM : (head + 1) * HEAD_DIM] = (total * SCALING).astype(BF16)


def add_sums(a_ref, b_ref, out_ref):
    out_ref[...] = a_ref[...].astype(F32) + b_ref[...].astype(F32)


def pack_sums(y_ref, near_ref, own_ref, back_ref, mine_ref, next_ref, prev_ref, far_ref, total):
    y = y_ref[0]
    total[...] = near_ref[...] + own_ref[...].astype(F32) + back_ref[...].astype(F32)
    for shift, ref in ((0, mine_ref), (1, next_ref), (3, prev_ref), (2, far_ref)):
        target = lax.rem(y + shift, 4)
        ref[...] = total[pl.ds(pl.multiple_of(target * 2 * FEATS, 2 * FEATS), 2 * FEATS), :].astype(BF16)


def finish_keys(a_ref, b_ref, c_ref, d_ref, dk_ref, dv_ref):
    total = a_ref[...].astype(F32) + b_ref[...].astype(F32)
    total = total + c_ref[...].astype(F32) + d_ref[...].astype(F32)
    dk_ref[...] = total[0:FEATS].astype(BF16)
    dv_ref[...] = total[FEATS : 2 * FEATS].astype(BF16)


def shift(value, axis, size, amount):
    return lax.ppermute(value, axis, [(i, (i + amount) % size) for i in range(size)])


X = ("xa", "xb")
Z = ("zh", "zl")


def per_device(queries, keys, values, outputs, d_out, lse):
    sds = jax.ShapeDtypeStruct
    y = lax.axis_index("y").astype(jnp.int32).reshape(1)
    core = lax.axis_index("c").astype(jnp.int32).reshape(1)
    y, core = lax.optimization_barrier((y, core))

    msg, kvt = pl.pallas_call(
        prepare,
        out_shape=(sds((8, MSG, HEAD_DIM), BF16), sds((2 * FEATS, KEYS), BF16)),
        in_specs=[pl.BlockSpec(memory_space=pl.ANY)] * 6,
        out_specs=(VMEM, VMEM),
        scratch_shapes=[pltpu.VMEM((ROWS, 2 * HEAD_DIM), BF16)] * 3
        + [pltpu.VMEM((2, ROWS), F32), pltpu.SemaphoreType.DMA((6,))],
        cost_estimate=pl.CostEstimate(flops=0, bytes_accessed=2**20, transcendentals=0),
        name="prepare",
    )(queries, d_out, outputs, lse, keys.T, values.T)
    q_own = lax.all_to_all(msg, Z, 0, 0, tiled=True)
    kv_next = shift(kvt, "y", 4, 3)
    kv_prev = shift(kvt, "y", 4, 1)
    kv_far = shift(kvt, "y", 4, 2)
    kv_own = call(
        join_keys,
        sds((2, KEYS, HEAD_DIM), BF16),
        [y, kvt, kv_next, kv_prev, kv_far],
        "join_keys",
        flops=20 * 2**30,
        scratch=[pltpu.VMEM((HEAD_DIM, KEYS), BF16)] * 2,
        scalars=1,
    )
    kv_x_prev = shift(kv_own, X, 4, 1)
    kv_x_next = shift(kv_own, X, 4, 3)
    kv_x_far = shift(kv_own, X, 4, 2)
    q_own, kv_x_prev, kv_x_next = lax.optimization_barrier((q_own, kv_x_prev, kv_x_next))
    q_other = shift(q_own, "c", 2, 1)

    msgs = [q_own, q_other]
    dq, sums_prev = attend_call(msgs, kv_x_prev, None, "attend_prev")
    back_prev = shift(sums_prev, X, 4, 3)
    dq, sums_next = attend_call(msgs, kv_x_next, dq, "attend_next")
    back_next = shift(sums_next, X, 4, 1)
    dq, sums_far = attend_call(msgs, kv_x_far, dq, "attend_far")
    back_far = shift(sums_far, X, 4, 2)
    dq, sums_own = attend_call(msgs, kv_own, dq, "attend_own", core=core)
    dq, back_prev = lax.optimization_barrier((dq, back_prev))
    dq = lax.all_to_all(dq, Z + ("c",), 0, 0, tiled=True)

    near = call(
        add_sums,
        sds((8 * FEATS, KEYS), F32),
        [back_prev, back_next],
        "add_sums",
        flops=2**37,
    )
    mine, to_next, to_prev, to_far = call(
        pack_sums,
        (sds((2 * FEATS, KEYS), BF16),) * 4,
        [y, near, sums_own, back_far],
        "pack_sums",
        scratch=[pltpu.VMEM((8 * FEATS, KEYS), F32)],
        scalars=1,
    )
    sums = [mine, shift(to_next, "y", 4, 1), shift(to_prev, "y", 4, 3), shift(to_far, "y", 4, 2)]
    d_queries = call(finish_queries, sds((ROWS, 2 * HEAD_DIM), BF16), [dq], "finish_queries")
    d_keys, d_values = call(
        finish_keys, (sds((FEATS, KEYS), BF16),) * 2, sums, "finish_keys"
    )
    return d_queries, d_keys.T, d_values.T


def solution(mesh):
    every = ("zh", "y", "zl", "xa", "xb", "c")
    fine = Mesh(mesh.devices.reshape(2, 4, 4, 2, 2, 2), every)
    blocks = P(("zl", "xa", "xb", "c"), ("zh", "y"))
    rows = P(every, None)
    return jax.shard_map(
        per_device,
        mesh=fine,
        in_specs=(rows, blocks, blocks, rows, rows, P(None, every)),
        out_specs=(rows, blocks, blocks),
        check_vma=False,
    )
```

```python
import functools
import math

import jax
import jax.numpy as jnp
from jax import lax
from jax.experimental import pallas as pl
from jax.experimental.pallas import tpu as pltpu
from jax.sharding import Mesh
from jax.sharding import PartitionSpec as P

F32 = jnp.float32
BF16 = jnp.bfloat16
HEAD_DIM = 128
ROWS = 128
KEYS = 1024
FEATS = 32
SIDE = 8
MSG = 2 * ROWS + SIDE
SCALING = HEAD_DIM ** (-0.5)
LOG2E = math.log2(math.e)
NT = (((1,), (1,)), ((), ()))
NN = (((1,), (0,)), ((), ()))
TN = (((0,), (0,)), ((), ()))
VMEM = pl.BlockSpec(memory_space=pltpu.VMEM)
SMEM = pl.BlockSpec(memory_space=pltpu.SMEM)


def dot(left, right, dims):
    return lax.dot_general(left, right, dims, preferred_element_type=F32)


def split3(value):
    high = value.astype(BF16).astype(F32)
    middle = (value - high).astype(BF16).astype(F32)
    return high, middle, value - high - middle


def call(body, out_shape, operands, name, flops=0, moved=1024, scratch=(), aliases=None, scalars=0, limit=8):
    return pl.pallas_call(
        body,
        out_shape=out_shape,
        in_specs=[SMEM] * scalars + [VMEM] * (len(operands) - scalars),
        out_specs=jax.tree.map(lambda _: VMEM, out_shape),
        scratch_shapes=list(scratch),
        input_output_aliases=aliases or {},
        compiler_params=pltpu.CompilerParams(vmem_limit_bytes=limit * 2**20),
        cost_estimate=pl.CostEstimate(flops=flops, bytes_accessed=moved, transcendentals=0),
        name=name,
    )(*operands)


def prepare(q_hbm, do_hbm, o_hbm, lse_hbm, k_hbm, v_hbm, msg_ref, kv_ref, q_s, do_s, o_s, lse_s, sems):
    copies = [
        pltpu.make_async_copy(do_hbm, do_s, sems.at[0]),
        pltpu.make_async_copy(o_hbm, o_s, sems.at[1]),
        pltpu.make_async_copy(lse_hbm, lse_s, sems.at[2]),
        pltpu.make_async_copy(q_hbm, q_s, sems.at[3]),
        pltpu.make_async_copy(k_hbm, kv_ref.at[pl.ds(0, FEATS)], sems.at[4]),
        pltpu.make_async_copy(v_hbm, kv_ref.at[pl.ds(FEATS, FEATS)], sems.at[5]),
    ]
    for copy in copies:
        copy.start()
    for copy in copies[:4]:
        copy.wait()
    product = do_s[...].astype(F32) * o_s[...].astype(F32)
    row = lax.broadcasted_iota(jnp.int32, (SIDE, ROWS), 0)
    for head in range(2):
        cols = pl.ds(head * HEAD_DIM, HEAD_DIM)
        part = product[:, head * HEAD_DIM : (head + 1) * HEAD_DIM]
        delta = jnp.sum(part.T, axis=0, keepdims=True)
        terms = split3(lse_s[head : head + 1, :] * LOG2E) + split3(delta)
        side = jnp.zeros((SIDE, ROWS), F32)
        for index, term in enumerate(terms):
            side = jnp.where(row == index, jnp.broadcast_to(term, (SIDE, ROWS)), side)
        side = side.astype(BF16)
        for place in range(4):
            target = head * 4 + place
            msg_ref[target, 0:ROWS, :] = q_s[:, cols]
            msg_ref[target, ROWS : 2 * ROWS, :] = do_s[:, cols]
            msg_ref[target, 2 * ROWS : MSG, :] = side
    for copy in copies[4:]:
        copy.wait()


def join_keys(y_ref, own_ref, next_ref, prev_ref, far_ref, kv_ref, kt, vt):
    y = y_ref[0]
    for shift, ref in ((0, own_ref), (3, prev_ref), (1, next_ref), (2, far_ref)):
        source = lax.rem(y + shift, 4)
        rows = pl.ds(pl.multiple_of(source * FEATS, FEATS), FEATS)
        kt[rows, :] = ref[0:FEATS, :]
        vt[rows, :] = ref[FEATS : 2 * FEATS, :]
    kv_ref[0] = kt[...].T
    kv_ref[1] = vt[...].T


def attend(first, last, *refs):
    refs = list(refs)
    core_ref = refs.pop(0) if last else None
    msg_refs = [refs.pop(0), refs.pop(0)]
    kv_ref = refs.pop(0)
    dq_in = None if first else refs.pop(0)
    dq_out = refs.pop(0)
    sums_ref, dk_s, dv_s = refs
    core = core_ref[0] if last else None
    key, value = kv_ref[0], kv_ref[1]

    def pair(msg_ref, place, start, size):
        return jnp.concatenate(
            [msg_ref[place, start : start + size, :], msg_ref[place + 1, start : start + size, :]],
            axis=0 if size == ROWS else 1,
        )

    for block in range(8):
        which, place = block % 2, block - block % 2
        msg_ref = msg_refs[which]
        query, grad = pair(msg_ref, place, 0, ROWS), pair(msg_ref, place, ROWS, ROWS)
        side = pair(msg_ref, place, 2 * ROWS, SIDE).astype(F32)
        lse = side[0:1] + side[1:2] + side[2:3]
        delta = side[3:4] + side[4:5] + side[5:6]
        scores = dot(key, query, NT)
        probs = jnp.exp2(scores * (SCALING * LOG2E) - lse)
        grad_probs = dot(value, grad, NT)
        grad_scores = (probs * (grad_probs - delta)).astype(BF16)
        dv = dot(probs.astype(BF16), grad, NN)
        dk = dot(grad_scores, query, NN)
        dv_s[...] = dv if block == 0 else dv_s[...] + dv
        dk_s[...] = dk if block == 0 else dk_s[...] + dk
        start = (which * 8 + place) * ROWS
        dq = dot(grad_scores, key, TN)
        if not first:
            dq = dq_in[start : start + 2 * ROWS, :] + dq
        if last:
            side_core = core if which == 0 else 1 - core
            dq_out[2 * place + side_core] = dq[:ROWS].astype(BF16)
            dq_out[2 * place + 2 + side_core] = dq[ROWS:].astype(BF16)
        else:
            dq_out[start : start + 2 * ROWS, :] = dq
    dk = (dk_s[...] * SCALING).astype(BF16).T
    dv = dv_s[...].astype(BF16).T
    for y in range(4):
        rows = slice(y * FEATS, (y + 1) * FEATS)
        sums_ref[2 * y * FEATS : (2 * y + 1) * FEATS, :] = dk[rows]
        sums_ref[(2 * y + 1) * FEATS : (2 * y + 2) * FEATS, :] = dv[rows]


def attend_call(msgs, chunk, dq_in, name, core=None):
    sds = jax.ShapeDtypeStruct
    first = dq_in is None
    last = core is not None
    operands = ([core] if last else []) + list(msgs) + [chunk] + ([] if first else [dq_in])
    if last:
        out = (sds((16, ROWS, HEAD_DIM), BF16),)
    else:
        out = (sds((16 * ROWS, HEAD_DIM), F32),)
    out += (sds((8 * FEATS, KEYS), BF16),)
    return call(
        functools.partial(attend, first, last),
        out,
        operands,
        name,
        moved=0,
        scratch=[pltpu.VMEM((KEYS, HEAD_DIM), F32)] * 2,
        scalars=int(last),
        limit=30,
    )


def finish_queries(in_ref, out_ref):
    for head in range(2):
        total = in_ref[head * 8].astype(F32)
        for place in range(1, 8):
            total = total + in_ref[head * 8 + place].astype(F32)
        out_ref[:, head * HEAD_DIM : (head + 1) * HEAD_DIM] = (total * SCALING).astype(BF16)


def add_sums(a_ref, b_ref, out_ref):
    out_ref[...] = a_ref[...].astype(F32) + b_ref[...].astype(F32)


def pack_sums(y_ref, near_ref, own_ref, back_ref, mine_ref, next_ref, prev_ref, far_ref, total):
    y = y_ref[0]
    total[...] = near_ref[...] + own_ref[...].astype(F32) + back_ref[...].astype(F32)
    for shift, ref in ((0, mine_ref), (1, next_ref), (3, prev_ref), (2, far_ref)):
        target = lax.rem(y + shift, 4)
        ref[...] = total[pl.ds(pl.multiple_of(target * 2 * FEATS, 2 * FEATS), 2 * FEATS), :].astype(BF16)


def finish_keys(a_ref, b_ref, c_ref, d_ref, dk_ref, dv_ref):
    total = a_ref[...].astype(F32) + b_ref[...].astype(F32)
    total = total + c_ref[...].astype(F32) + d_ref[...].astype(F32)
    dk_ref[...] = total[0:FEATS].astype(BF16)
    dv_ref[...] = total[FEATS : 2 * FEATS].astype(BF16)


def shift(value, axis, size, amount):
    return lax.ppermute(value, axis, [(i, (i + amount) % size) for i in range(size)])


X = ("xa", "xb")
Z = ("zh", "zl")


def per_device(queries, keys, values, outputs, d_out, lse):
    sds = jax.ShapeDtypeStruct
    y = lax.axis_index("y").astype(jnp.int32).reshape(1)
    core = lax.axis_index("c").astype(jnp.int32).reshape(1)
    y, core = lax.optimization_barrier((y, core))

    msg, kvt = pl.pallas_call(
        prepare,
        out_shape=(sds((8, MSG, HEAD_DIM), BF16), sds((2 * FEATS, KEYS), BF16)),
        in_specs=[pl.BlockSpec(memory_space=pl.ANY)] * 6,
        out_specs=(VMEM, VMEM),
        scratch_shapes=[pltpu.VMEM((ROWS, 2 * HEAD_DIM), BF16)] * 3
        + [pltpu.VMEM((2, ROWS), F32), pltpu.SemaphoreType.DMA((6,))],
        cost_estimate=pl.CostEstimate(flops=0, bytes_accessed=2**20, transcendentals=0),
        name="prepare",
    )(queries, d_out, outputs, lse, keys.T, values.T)
    q_own = lax.all_to_all(msg, Z, 0, 0, tiled=True)
    kv_next = shift(kvt, "y", 4, 3)
    kv_prev = shift(kvt, "y", 4, 1)
    kv_far = shift(kvt, "y", 4, 2)
    kv_own = call(
        join_keys,
        sds((2, KEYS, HEAD_DIM), BF16),
        [y, kvt, kv_next, kv_prev, kv_far],
        "join_keys",
        flops=20 * 2**30,
        scratch=[pltpu.VMEM((HEAD_DIM, KEYS), BF16)] * 2,
        scalars=1,
    )
    kv_x_prev = shift(kv_own, X, 4, 1)
    kv_x_next = shift(kv_own, X, 4, 3)
    kv_x_far = shift(kv_own, X, 4, 2)
    q_own, kv_x_prev, kv_x_next = lax.optimization_barrier((q_own, kv_x_prev, kv_x_next))
    q_other = shift(q_own, "c", 2, 1)

    msgs = [q_own, q_other]
    dq, sums_prev = attend_call(msgs, kv_x_prev, None, "attend_prev")
    back_prev = shift(sums_prev, X, 4, 3)
    dq, sums_next = attend_call(msgs, kv_x_next, dq, "attend_next")
    back_next = shift(sums_next, X, 4, 1)
    dq, sums_far = attend_call(msgs, kv_x_far, dq, "attend_far")
    back_far = shift(sums_far, X, 4, 2)
    dq, sums_own = attend_call(msgs, kv_own, dq, "attend_own", core=core)
    dq, back_prev = lax.optimization_barrier((dq, back_prev))
    dq = lax.all_to_all(dq, Z + ("c",), 0, 0, tiled=True)

    near = call(
        add_sums,
        sds((8 * FEATS, KEYS), F32),
        [back_prev, back_next],
        "add_sums",
        flops=2**37,
    )
    mine, to_next, to_prev, to_far = call(
        pack_sums,
        (sds((2 * FEATS, KEYS), BF16),) * 4,
        [y, near, sums_own, back_far],
        "pack_sums",
        scratch=[pltpu.VMEM((8 * FEATS, KEYS), F32)],
        scalars=1,
    )
    sums = [mine, shift(to_next, "y", 4, 1), shift(to_prev, "y", 4, 3), shift(to_far, "y", 4, 2)]
    d_queries = call(finish_queries, sds((ROWS, 2 * HEAD_DIM), BF16), [dq], "finish_queries")
    d_keys, d_values = call(
        finish_keys, (sds((FEATS, KEYS), BF16),) * 2, sums, "finish_keys"
    )
    return d_queries, d_keys.T, d_values.T


def solution(mesh):
    every = ("zh", "y", "zl", "xa", "xb", "c")
    fine = Mesh(mesh.devices.reshape(2, 4, 4, 2, 2, 2), every)
    blocks = P(("zl", "xa", "xb", "c"), ("zh", "y"))
    rows = P(every, None)
    return jax.shard_map(
        per_device,
        mesh=fine,
        in_specs=(rows, blocks, blocks, rows, rows, P(None, every)),
        out_specs=(rows, blocks, blocks),
        check_vma=False,
    )
```

```python
import functools
import math

import jax
import jax.numpy as jnp
from jax import lax
from jax.experimental import pallas as pl
from jax.experimental.pallas import tpu as pltpu
from jax.sharding import Mesh
from jax.sharding import PartitionSpec as P

F32 = jnp.float32
BF16 = jnp.bfloat16
HEAD_DIM = 128
ROWS = 128
KEYS = 1024
FEATS = 32
SIDE = 8
MSG = 2 * ROWS + SIDE
SCALING = HEAD_DIM ** (-0.5)
LOG2E = math.log2(math.e)
NT = (((1,), (1,)), ((), ()))
NN = (((1,), (0,)), ((), ()))
TN = (((0,), (0,)), ((), ()))
VMEM = pl.BlockSpec(memory_space=pltpu.VMEM)
SMEM = pl.BlockSpec(memory_space=pltpu.SMEM)


def dot(left, right, dims):
    return lax.dot_general(left, right, dims, preferred_element_type=F32)


def split3(value):
    high = value.astype(BF16).astype(F32)
    middle = (value - high).astype(BF16).astype(F32)
    return high, middle, value - high - middle


def call(body, out_shape, operands, name, flops=0, moved=1024, scratch=(), aliases=None, scalars=0, limit=8):
    return pl.pallas_call(
        body,
        out_shape=out_shape,
        in_specs=[SMEM] * scalars + [VMEM] * (len(operands) - scalars),
        out_specs=jax.tree.map(lambda _: VMEM, out_shape),
        scratch_shapes=list(scratch),
        input_output_aliases=aliases or {},
        compiler_params=pltpu.CompilerParams(vmem_limit_bytes=limit * 2**20),
        cost_estimate=pl.CostEstimate(flops=flops, bytes_accessed=moved, transcendentals=0),
        name=name,
    )(*operands)


def prepare(q_hbm, do_hbm, o_hbm, lse_hbm, k_hbm, v_hbm, msg_ref, kv_ref, q_s, do_s, o_s, lse_s, sems):
    copies = [
        pltpu.make_async_copy(do_hbm, do_s, sems.at[0]),
        pltpu.make_async_copy(o_hbm, o_s, sems.at[1]),
        pltpu.make_async_copy(lse_hbm, lse_s, sems.at[2]),
        pltpu.make_async_copy(q_hbm, q_s, sems.at[3]),
        pltpu.make_async_copy(k_hbm, kv_ref.at[pl.ds(0, FEATS)], sems.at[4]),
        pltpu.make_async_copy(v_hbm, kv_ref.at[pl.ds(FEATS, FEATS)], sems.at[5]),
    ]
    for copy in copies:
        copy.start()
    for copy in copies[:4]:
        copy.wait()
    product = do_s[...].astype(F32) * o_s[...].astype(F32)
    row = lax.broadcasted_iota(jnp.int32, (SIDE, ROWS), 0)
    for head in range(2):
        cols = pl.ds(head * HEAD_DIM, HEAD_DIM)
        part = product[:, head * HEAD_DIM : (head + 1) * HEAD_DIM]
        delta = jnp.sum(part.T, axis=0, keepdims=True)
        terms = split3(lse_s[head : head + 1, :] * LOG2E) + split3(delta)
        side = jnp.zeros((SIDE, ROWS), F32)
        for index, term in enumerate(terms):
            side = jnp.where(row == index, jnp.broadcast_to(term, (SIDE, ROWS)), side)
        side = side.astype(BF16)
        for place in range(4):
            target = head * 4 + place
            msg_ref[target, 0:ROWS, :] = q_s[:, cols]
            msg_ref[target, ROWS : 2 * ROWS, :] = do_s[:, cols]
            msg_ref[target, 2 * ROWS : MSG, :] = side
    for copy in copies[4:]:
        copy.wait()


def join_keys(y_ref, own_ref, next_ref, prev_ref, far_ref, kv_ref, kt, vt):
    y = y_ref[0]
    for shift, ref in ((0, own_ref), (3, prev_ref), (1, next_ref), (2, far_ref)):
        source = lax.rem(y + shift, 4)
        rows = pl.ds(pl.multiple_of(source * FEATS, FEATS), FEATS)
        kt[rows, :] = ref[0:FEATS, :]
        vt[rows, :] = ref[FEATS : 2 * FEATS, :]
    kv_ref[0] = kt[...].T
    kv_ref[1] = vt[...].T


def attend(first, last, *refs):
    refs = list(refs)
    core_ref = refs.pop(0) if last else None
    msg_refs = [refs.pop(0), refs.pop(0)]
    kv_ref = refs.pop(0)
    dq_in = None if first else refs.pop(0)
    dq_out = refs.pop(0)
    sums_ref, dk_s, dv_s = refs
    core = core_ref[0] if last else None
    key, value = kv_ref[0], kv_ref[1]

    def pair(msg_ref, place, start, size):
        return jnp.concatenate(
            [msg_ref[place, start : start + size, :], msg_ref[place + 1, start : start + size, :]],
            axis=0 if size == ROWS else 1,
        )

    for block in range(8):
        which, place = block % 2, block - block % 2
        msg_ref = msg_refs[which]
        query, grad = pair(msg_ref, place, 0, ROWS), pair(msg_ref, place, ROWS, ROWS)
        side = pair(msg_ref, place, 2 * ROWS, SIDE).astype(F32)
        lse = side[0:1] + side[1:2] + side[2:3]
        delta = side[3:4] + side[4:5] + side[5:6]
        scores = dot(key, query, NT)
        probs = jnp.exp2(scores * (SCALING * LOG2E) - lse)
        grad_probs = dot(value, grad, NT)
        grad_scores = (probs * (grad_probs - delta)).astype(BF16)
        dv = dot(probs.astype(BF16), grad, NN)
        dk = dot(grad_scores, query, NN)
        dv_s[...] = dv if block == 0 else dv_s[...] + dv
        dk_s[...] = dk if block == 0 else dk_s[...] + dk
        start = (which * 8 + place) * ROWS
        dq = dot(grad_scores, key, TN)
        if not first:
            dq = dq_in[start : start + 2 * ROWS, :] + dq
        if last:
            side_core = core if which == 0 else 1 - core
            dq_out[2 * place + side_core] = dq[:ROWS].astype(BF16)
            dq_out[2 * place + 2 + side_core] = dq[ROWS:].astype(BF16)
        else:
            dq_out[start : start + 2 * ROWS, :] = dq
    dk = (dk_s[...] * SCALING).astype(BF16).T
    dv = dv_s[...].astype(BF16).T
    for y in range(4):
        rows = slice(y * FEATS, (y + 1) * FEATS)
        sums_ref[2 * y * FEATS : (2 * y + 1) * FEATS, :] = dk[rows]
        sums_ref[(2 * y + 1) * FEATS : (2 * y + 2) * FEATS, :] = dv[rows]


def attend_call(msgs, chunk, dq_in, name, core=None):
    sds = jax.ShapeDtypeStruct
    first = dq_in is None
    last = core is not None
    operands = ([core] if last else []) + list(msgs) + [chunk] + ([] if first else [dq_in])
    if last:
        out = (sds((16, ROWS, HEAD_DIM), BF16),)
    else:
        out = (sds((16 * ROWS, HEAD_DIM), F32),)
    out += (sds((8 * FEATS, KEYS), BF16),)
    return call(
        functools.partial(attend, first, last),
        out,
        operands,
        name,
        moved=0,
        scratch=[pltpu.VMEM((KEYS, HEAD_DIM), F32)] * 2,
        scalars=int(last),
        limit=30,
    )


def finish_queries(in_ref, out_ref):
    for head in range(2):
        total = in_ref[head * 8].astype(F32)
        for place in range(1, 8):
            total = total + in_ref[head * 8 + place].astype(F32)
        out_ref[:, head * HEAD_DIM : (head + 1) * HEAD_DIM] = (total * SCALING).astype(BF16)


def add_sums(a_ref, b_ref, out_ref):
    out_ref[...] = a_ref[...].astype(F32) + b_ref[...].astype(F32)


def pack_sums(y_ref, near_ref, own_ref, back_ref, mine_ref, next_ref, prev_ref, far_ref, total):
    y = y_ref[0]
    total[...] = near_ref[...] + own_ref[...].astype(F32) + back_ref[...].astype(F32)
    for shift, ref in ((0, mine_ref), (1, next_ref), (3, prev_ref), (2, far_ref)):
        target = lax.rem(y + shift, 4)
        ref[...] = total[pl.ds(pl.multiple_of(target * 2 * FEATS, 2 * FEATS), 2 * FEATS), :].astype(BF16)


def finish_keys(a_ref, b_ref, c_ref, d_ref, dk_ref, dv_ref):
    total = a_ref[...].astype(F32) + b_ref[...].astype(F32)
    total = total + c_ref[...].astype(F32) + d_ref[...].astype(F32)
    dk_ref[...] = total[0:FEATS].astype(BF16)
    dv_ref[...] = total[FEATS : 2 * FEATS].astype(BF16)


def shift(value, axis, size, amount):
    return lax.ppermute(value, axis, [(i, (i + amount) % size) for i in range(size)])


X = ("xa", "xb")
Z = ("zh", "zl")


def per_device(queries, keys, values, outputs, d_out, lse):
    sds = jax.ShapeDtypeStruct
    y = lax.axis_index("y").astype(jnp.int32).reshape(1)
    core = lax.axis_index("c").astype(jnp.int32).reshape(1)
    y, core = lax.optimization_barrier((y, core))

    msg, kvt = pl.pallas_call(
        prepare,
        out_shape=(sds((8, MSG, HEAD_DIM), BF16), sds((2 * FEATS, KEYS), BF16)),
        in_specs=[pl.BlockSpec(memory_space=pl.ANY)] * 6,
        out_specs=(VMEM, VMEM),
        scratch_shapes=[pltpu.VMEM((ROWS, 2 * HEAD_DIM), BF16)] * 3
        + [pltpu.VMEM((2, ROWS), F32), pltpu.SemaphoreType.DMA((6,))],
        cost_estimate=pl.CostEstimate(flops=0, bytes_accessed=2**20, transcendentals=0),
        name="prepare",
    )(queries, d_out, outputs, lse, keys.T, values.T)
    q_own = lax.all_to_all(msg, Z, 0, 0, tiled=True)
    kv_next = shift(kvt, "y", 4, 3)
    kv_prev = shift(kvt, "y", 4, 1)
    kv_far = shift(kvt, "y", 4, 2)
    kv_own = call(
        join_keys,
        sds((2, KEYS, HEAD_DIM), BF16),
        [y, kvt, kv_next, kv_prev, kv_far],
        "join_keys",
        flops=20 * 2**30,
        scratch=[pltpu.VMEM((HEAD_DIM, KEYS), BF16)] * 2,
        scalars=1,
    )
    kv_x_prev = shift(kv_own, X, 4, 1)
    kv_x_next = shift(kv_own, X, 4, 3)
    kv_x_far = shift(kv_own, X, 4, 2)
    q_own, kv_x_prev, kv_x_next = lax.optimization_barrier((q_own, kv_x_prev, kv_x_next))
    q_other = shift(q_own, "c", 2, 1)

    msgs = [q_own, q_other]
    dq, sums_prev = attend_call(msgs, kv_x_prev, None, "attend_prev")
    back_prev = shift(sums_prev, X, 4, 3)
    dq, sums_next = attend_call(msgs, kv_x_next, dq, "attend_next")
    back_next = shift(sums_next, X, 4, 1)
    dq, sums_far = attend_call(msgs, kv_x_far, dq, "attend_far")
    back_far = shift(sums_far, X, 4, 2)
    dq, sums_own = attend_call(msgs, kv_own, dq, "attend_own", core=core)
    dq, back_prev = lax.optimization_barrier((dq, back_prev))
    dq = lax.all_to_all(dq, Z + ("c",), 0, 0, tiled=True)

    near = call(
        add_sums,
        sds((8 * FEATS, KEYS), F32),
        [back_prev, back_next],
        "add_sums",
        flops=2**37,
    )
    mine, to_next, to_prev, to_far = call(
        pack_sums,
        (sds((2 * FEATS, KEYS), BF16),) * 4,
        [y, near, sums_own, back_far],
        "pack_sums",
        scratch=[pltpu.VMEM((8 * FEATS, KEYS), F32)],
        scalars=1,
    )
    sums = [mine, shift(to_far, "y", 4, 2), shift(to_next, "y", 4, 1), shift(to_prev, "y", 4, 3)]
    d_queries = call(finish_queries, sds((ROWS, 2 * HEAD_DIM), BF16), [dq], "finish_queries")
    d_keys, d_values = call(
        finish_keys, (sds((FEATS, KEYS), BF16),) * 2, sums, "finish_keys"
    )
    return d_queries, d_keys.T, d_values.T


def solution(mesh):
    every = ("zh", "y", "zl", "xa", "xb", "c")
    fine = Mesh(mesh.devices.reshape(2, 4, 4, 2, 2, 2), every)
    blocks = P(("zl", "xa", "xb", "c"), ("zh", "y"))
    rows = P(every, None)
    return jax.shard_map(
        per_device,
        mesh=fine,
        in_specs=(rows, blocks, blocks, rows, rows, P(None, every)),
        out_specs=(rows, blocks, blocks),
        check_vma=False,
    )
```
